32 devices in a mesh: tm: 4 (over z), space: 8 (over y, x, core).
Axes of the slice: x: 2, y: 2, z: 4, core: 2. Of those that a mesh axis runs over, the one named last changes fastest.
Arguments:
- labels: int32 [32, 64, 256], P('space'), may hold values from 0 to 3
- conductivity: float32 [4], replicated, may hold values from 0.02 to 1
- coil_pattern: float32 [3, 32, 64, 256], P(None, 'space'), may hold values from -18 to 18
- currents: float32 [4, 2, 3], P('tm'), may hold values from -4 to 4
- initial_state: float32 [32, 64, 256], P('space'), may hold values from -6 to 6
Outputs:
- slice_starts: float32 [4, 32, 64, 256], P('tm', 'space')
- fine_ends: float32 [4, 32, 64, 256], P('tm', 'space')
The draws below stay inside these ranges and needn't reach their ends.
All inputs are finite; a program needn't handle non-finite values.
Results may differ from the reference program's by a relative error of at most 0.00021.
Values sent between devices are 32-bit elements; how exact they have to be, the bound alone decides.
A program may use at most 64 MiB of HBM per device.

```python
import math
import jax
import jax.numpy as jnp

NY = 64
NZ = 256
REGIONS = 4
PHASES = 3
FINE_STEPS = 2
CG_FINE = 2
CG_COARSE = 4
PARA_ITERS = 2
SLICES = 4
NX = 32


def draw_coil_pattern(key, part):
    shape = (PHASES, NX, NY, NZ)
    rows = jnp.arange(NX, dtype=jnp.float32) / max(NX - 1, 1)
    noise = jax.random.truncated_normal(key, -4.0, 4.0, shape, jnp.float32)
    return noise * (3.0 ** rows)[None, :, None, None]


def with_ends(entries, stream_key, low, high):
    shape = entries.shape
    index_at = [jax.random.randint(jax.random.fold_in(stream_key, axis), (), 0, shape[axis]) for axis in range(len(shape))]
    entries = entries.at[tuple(index_at)].set(low)
    longest = shape.index(max(shape))
    index_at[longest] = (index_at[longest] + 1) % shape[longest]
    return entries.at[tuple(index_at)].set(high)


def block_scale(own_key, shape, cuts, least, high):
    def one(axis_at, shards_of):
        heights = jax.random.uniform(jax.random.fold_in(jax.random.fold_in(own_key, 6), axis_at), (shards_of,), jnp.float32, least / len(cuts), high / len(cuts))
        return jnp.repeat(jnp.exp(heights), shape[axis_at] // shards_of).reshape((-1,) + (1,) * (len(shape) - axis_at - 1))

    factor_of = one(*cuts[0])
    for cut in cuts[1:]:
        factor_of = factor_of * one(*cut)
    return factor_of


def gaussian(own_key, dims, deviation, limit, pieces=(), kind=jnp.bfloat16):
    factor_of = block_scale(own_key, dims, pieces, -0.22, 0.18) if pieces else 1.0
    array = jax.random.normal(own_key, dims, jnp.float32) * deviation * factor_of
    return jnp.minimum(jnp.maximum(array, -limit), limit).astype(kind)


def setup_inputs(seed: int = 0) -> dict:
    key_list = jax.random.split(jax.random.key(seed), 6)
    return {
        "labels": with_ends(jax.random.randint(key_list[0], (NX, NY, NZ), 0, REGIONS), jax.random.fold_in(key_list[0], 1), 0, REGIONS - 1).astype(jnp.int32),
        "conductivity": jnp.clip(jnp.exp(jax.random.uniform(key_list[1], (REGIONS,), jnp.float32, math.log(0.02), math.log(1.0))), 0.02, 1.0),
        "coil_pattern": draw_coil_pattern(jax.random.fold_in(key_list[5], 71), 0),
        "currents": gaussian(key_list[3], (SLICES, FINE_STEPS, PHASES), 1.0, 4.0, ((0, 4),), jnp.float32),
        "initial_state": gaussian(key_list[4], (NX, NY, NZ), 1.0, 6.0, ((0, 8),), jnp.float32),
    }


def restrict(volume):
    first_dim, second_dim, third_dim = volume.shape
    blocks = volume.reshape(first_dim // 4, 4, second_dim // 4, 4, third_dim // 4, 4)
    return jnp.mean(blocks, axis=(1, 3, 5))


def prolong(coarse_field):
    first_dim, second_dim, third_dim = coarse_field.shape
    spread = jnp.broadcast_to(coarse_field[:, None, :, None, :, None], (first_dim, 4, second_dim, 4, third_dim, 4))
    return spread.reshape(first_dim * 4, second_dim * 4, third_dim * 4)


def neighbours(padded):
    summed = padded[2:, 1:-1, 1:-1] + padded[:-2, 1:-1, 1:-1]
    summed = summed + padded[1:-1, 2:, 1:-1] + padded[1:-1, :-2, 1:-1]
    return summed + padded[1:-1, 1:-1, 2:] + padded[1:-1, 1:-1, :-2]


def fine_operator(volume, weight):
    beside = neighbours(jnp.pad(volume, 1))
    return weight * volume + (6.0 * volume - beside)


def coarse_operator(volume, weight):
    beside = neighbours(jnp.pad(volume, 1))
    return weight * volume + 0.0625 * (6.0 * volume - beside)


def conjugate(operator, right_side, guess, count):
    solution = guess
    residual = right_side - operator(solution)
    direction = residual
    res_norm = jnp.sum(residual * residual)
    for sweep_step in range(count):
        applied = operator(direction)
        step_len = res_norm / jnp.sum(direction * applied)
        solution = solution + step_len * direction
        residual = residual - step_len * applied
        if sweep_step + 1 < count:
            new_norm = jnp.sum(residual * residual)
            direction = residual + (new_norm / res_norm) * direction
            res_norm = new_norm
    return solution


def reference(labels, conductivity, coil_pattern, currents, initial_state):
    sigma_cell = conductivity[labels]
    sigma_coarse = restrict(sigma_cell)
    coils_coarse = jnp.stack([restrict(coil_pattern[phase_index]) for phase_index in range(PHASES)])
    weight_coarse = sigma_coarse / float(FINE_STEPS)

    def fine_run(slice_index, volume):
        for step_index in range(FINE_STEPS):
            source = currents[slice_index, step_index, 0] * coil_pattern[0]
            for phase_index in range(1, PHASES):
                source = source + currents[slice_index, step_index, phase_index] * coil_pattern[phase_index]
            right_side = sigma_cell * volume + source
            volume = conjugate(lambda vector_in: fine_operator(vector_in, sigma_cell), right_side, volume, CG_FINE)
        return volume

    def coarse_run(slice_index, volume):
        coarse_start = restrict(volume)
        mean_current = jnp.mean(currents[slice_index], axis=0)
        source = mean_current[0] * coils_coarse[0]
        for phase_index in range(1, PHASES):
            source = source + mean_current[phase_index] * coils_coarse[phase_index]
        right_side = weight_coarse * coarse_start + source
        solved = conjugate(lambda vector_in: coarse_operator(vector_in, weight_coarse), right_side, coarse_start, CG_COARSE)
        return prolong(solved)

    starts = [initial_state]
    coarse_out = []
    for slice_index in range(SLICES):
        coarse_out.append(coarse_run(slice_index, starts[slice_index]))
        starts.append(coarse_out[slice_index])
    fine_out = []
    for para_index in range(PARA_ITERS):
        fine_out = [fine_run(slice_index, starts[slice_index]) for slice_index in range(SLICES)]
        new_starts = [starts[SLICES]]
        new_coarse = []
        for slice_index in range(SLICES):
            coarse_result = coarse_run(slice_index, new_starts[slice_index])
            new_coarse.append(coarse_result)
            new_starts.append(coarse_result + fine_out[slice_index] - coarse_out[slice_index])
        starts = new_starts
        coarse_out = new_coarse
    return jnp.stack(starts[:SLICES]), jnp.stack(fine_out)
```

```python
import functools

import jax
import jax.numpy as jnp
from jax import lax
from jax.experimental import pallas as pl
from jax.experimental.pallas import tpu as pltpu
from jax.sharding import PartitionSpec as P

FINE_STEPS = 2
CG_COARSE = 4
PARA_ITERS = 2
MESH = pl.DeviceIdType.MESH
HIGH = lax.Precision.HIGHEST
F32 = jnp.float32


def dot(a, b):
    return lax.dot_general(
        a, b, (((1,), (0,)), ((), ())), precision=HIGH, preferred_element_type=F32
    )


def kernel(
    T, S, lx, labels, cond, coil, currents, init, starts_out, ends_out,
    cur, setup, wt, G, D, C, rf, arb, U, R, V, SRC, SIG, HL, HH, ZB, FE, send, recv,
):
    NY, NZ = init.shape[1], init.shape[2]
    px = lx // 4
    XC = S * px
    hr, hl = NY // 8, NZ // 4
    N = T * S
    n = lax.axis_index("tm")
    s = lax.axis_index("space")
    me = n * S + s
    has_lo, has_hi = s > 0, s < S - 1
    phases = coil.shape[0]

    def others(count, own, fn):
        def step(i, carry):
            fn(lax.rem(own + i, count))
            return carry

        lax.fori_loop(1, count, step, 0)

    barrier = pltpu.get_barrier_semaphore()
    others(
        N,
        me,
        lambda d: pl.semaphore_signal(
            barrier, inc=1, device_id=(d // S, lax.rem(d, S)), device_id_type=MESH
        ),
    )

    def remote(src, dst, i, dev):
        return pltpu.make_async_remote_copy(
            src_ref=src, dst_ref=dst, send_sem=send.at[i], recv_sem=recv.at[i],
            device_id=dev, device_id_type=MESH,
        )

    def wait_on(ref, sem):
        pltpu.make_async_copy(ref, ref, sem).wait()

    up_dev, down_dev = (n, s + 1), (n, s - 1)

    rowi = lax.broadcasted_iota(jnp.int32, (NY, NZ), 0)
    coli = lax.broadcasted_iota(jnp.int32, (NY, NZ), 1)
    ey = (lax.broadcasted_iota(jnp.int32, (NY // 4, NY), 1) // 4
          == lax.broadcasted_iota(jnp.int32, (NY // 4, NY), 0)).astype(F32)
    eyt = (lax.broadcasted_iota(jnp.int32, (NY, NY // 4), 0) // 4
           == lax.broadcasted_iota(jnp.int32, (NY, NY // 4), 1)).astype(F32)
    zr = lax.broadcasted_iota(jnp.int32, (NZ, 2 * hl), 0) // 4
    zc = lax.broadcasted_iota(jnp.int32, (NZ, 2 * hl), 1)
    down_lo = (zr == zc).astype(F32)
    down_hi = (zr == zc - hl).astype(F32)
    tr = lax.broadcasted_iota(jnp.int32, (2 * hl, NZ), 0)
    tc = lax.broadcasted_iota(jnp.int32, (2 * hl, NZ), 1) // 4
    up_lo = (tr == tc).astype(F32)
    up_hi = (tr - hl == tc).astype(F32)

    def restrict4(total):
        t = dot(ey, total)
        return (dot(t[:hr], down_lo) + dot(t[hr:], down_hi)) * (1.0 / 64.0)

    def prolong(c):
        t = jnp.concatenate([dot(c, up_lo), dot(c, up_hi)], axis=0)
        return dot(eyt, t)

    def beside_yz(x):
        a = jnp.where(rowi > 0, pltpu.roll(x, 1, 0), 0.0)
        b = jnp.where(rowi < NY - 1, pltpu.roll(x, NY - 1, 0), 0.0)
        c = jnp.where(coli > 0, pltpu.roll(x, 1, 1), 0.0)
        d = jnp.where(coli < NZ - 1, pltpu.roll(x, NZ - 1, 1), 0.0)
        return (a + b) + (c + d)

    for p in range(lx):
        lab = labels[p]
        sig = jnp.where(lab == 0, cond[0], 0.0)
        for region in range(1, cond.shape[0]):
            sig = jnp.where(lab == region, cond[region], sig)
        SIG[p] = sig
        for f in range(FINE_STEPS):
            src = currents[0, f, 0] * coil[0, p]
            for ph in range(1, phases):
                src = src + currents[0, f, ph] * coil[ph, p]
            SRC[f, p + 1] = src

    for b in range(px):
        def total(get):
            return (get(4 * b) + get(4 * b + 1)) + (get(4 * b + 2) + get(4 * b + 3))

        setup[s * px + b, 0] = restrict4(total(lambda p: init[p]))
        setup[s * px + b, 1] = restrict4(total(lambda p: SIG[p]))
        for ph in range(phases):
            setup[s * px + b, 2 + ph] = restrict4(total(lambda p, ph=ph: coil[ph, p]))
    row8 = lax.broadcasted_iota(jnp.int32, (8, 2 * hl), 0)
    mean = jnp.zeros((8, 2 * hl), F32)
    for ph in range(phases):
        m = currents[0, 0, ph]
        for f in range(1, FINE_STEPS):
            m = m + currents[0, f, ph]
        mean = jnp.where(row8 == ph, m / float(FINE_STEPS), mean)
    cur[n] = mean

    zero = jnp.zeros((NY, NZ), F32)

    @pl.when(jnp.logical_not(has_lo))
    def _():
        for ref, ids in ((HL, (0, 1)), (R, (0,)), (V, (0, 1)), (SRC.at[0], (0,)), (SRC.at[1], (0,))):
            for i in ids:
                ref[i] = zero

    @pl.when(jnp.logical_not(has_hi))
    def _():
        for ref, ids in (
            (HH, (0, 1, 2)), (R, (lx + 4,)), (V, (lx + 3, lx + 4)),
            (SRC.at[0], (lx + 1, lx + 2)), (SRC.at[1], (lx + 1, lx + 2)), (SIG, (lx,)),
        ):
            for i in ids:
                ref[i] = zero

    pl.semaphore_wait(barrier, N - 1)

    mine = setup.at[pl.ds(s * px, px)]
    others(S, s, lambda d: remote(mine, mine, 0, (n, d)).start())
    others(T, n, lambda d: remote(cur.at[n], cur.at[n], 1, (d, s)).start())
    c_src_up = remote(SRC.at[:, lx], SRC.at[:, 0], 2, up_dev)
    c_src_dn = remote(SRC.at[:, pl.ds(1, 2)], SRC.at[:, pl.ds(lx + 1, 2)], 3, down_dev)
    c_sig_dn = remote(SIG.at[0], SIG.at[lx], 4, down_dev)
    c_ini_up = remote(init.at[pl.ds(lx - 2, 2)], HL, 5, up_dev)
    c_ini_dn = remote(init.at[pl.ds(0, 3)], HH, 6, down_dev)
    first = n == 0
    up_copies = ((c_src_up, None),)
    down_copies = ((c_src_dn, None), (c_sig_dn, None))

    @pl.when(jnp.logical_and(first, has_hi))
    def _():
        c_ini_up.start()

    @pl.when(jnp.logical_and(first, has_lo))
    def _():
        c_ini_dn.start()

    @pl.when(has_hi)
    def _():
        c_src_up.start()

    @pl.when(has_lo)
    def _():
        c_src_dn.start()
        c_sig_dn.start()

    crow = lax.broadcasted_iota(jnp.int32, (XC, hr, 2 * hl), 1)
    ccol = lax.broadcasted_iota(jnp.int32, (XC, hr, 2 * hl), 2)
    cz = lax.rem(ccol, hl)
    zplane = jnp.zeros((1, hr, 2 * hl), F32)

    def coarse_lap(c):
        xs = jnp.concatenate([zplane, c[:-1]], 0) + jnp.concatenate([c[1:], zplane], 0)
        w = pltpu.roll(c, hl, 2)
        za = jnp.where(cz > 0, pltpu.roll(c, 1, 2), 0.0)
        zb = jnp.where(cz < hl - 1, pltpu.roll(c, 2 * hl - 1, 2), 0.0)
        ya = pltpu.roll(
            jnp.where(crow == hr - 1, jnp.where(ccol >= hl, w, 0.0), c), 1, 1)
        yb = pltpu.roll(
            jnp.where(crow == 0, jnp.where(ccol < hl, w, 0.0), c), hr - 1, 1)
        return 0.0625 * (6.0 * c - ((xs + za) + (zb + ya) + yb))

    def total3(x):
        return jnp.sum(jnp.sum(x, axis=0), keepdims=True).reshape(1, 1, 1)

    def solve(i, c):
        source = cur[i, 0:1, :][None] * setup[:, 2]
        for ph in range(1, phases):
            source = source + cur[i, ph:ph + 1, :][None] * setup[:, 2 + ph]
        weight = wt[...]
        r = source - coarse_lap(c)
        q = weight * r + coarse_lap(r)
        rr, rq = total3(r * r), total3(r * q)
        alpha = rr / rq
        d, x = r, c
        for it in range(CG_COARSE):
            x = x + alpha * d
            if it + 1 < CG_COARSE:
                r = r - alpha * q
                w = weight * r + coarse_lap(r)
                new, rw = total3(r * r), total3(r * w)
                beta = new / rr
                alpha = new / (rw - beta * new / alpha)
                d = r + beta * d
                q = w + beta * q
                rr = new
        return x

    def solve_step(i, k):
        g = solve(i, C[...])
        if k == 0:
            D[i] = g
            C[...] = g
        else:
            diff = g - G[i]
            D[i] = diff
        G[i] = g

    def next_start(i, k):
        C[...] = D[i] + rf[k - 1, pl.ds(i * XC, XC)]

    def fine_residual(f):
        def step(i, carry):
            g = s * lx + i - 1
            u = U[i + 1]
            r = SRC[f, i] - 6.0 * u + ((U[i] + U[i + 2]) + beside_yz(u))
            inside = jnp.logical_and(g >= 0, g < S * lx)
            R[i + 1] = jnp.where(inside, r, 0.0)
            return carry

        lax.fori_loop(0, lx + 3, step, 0)

        def step_v(i, carry):
            g = s * lx + i
            r = R[i + 2]
            v = (SIG[i] + 6.0) * r - ((R[i + 1] + R[i + 3]) + beside_yz(r))
            V[i + 2] = jnp.where(g < S * lx, v, 0.0)
            return carry

        lax.fori_loop(0, lx + 1, step_v, 0)

    def fold(x):
        y = x[:, :2 * hl]
        for j in range(1, NZ // (2 * hl)):
            y = y + x[:, 2 * hl * j:2 * hl * (j + 1)]
        z = y[:8]
        for j in range(1, NY // 8):
            z = z + y[8 * j:8 * (j + 1)]
        return z

    def fine_moments(stage):
        def step(i, carry):
            m0, m1, m2, m3 = carry
            r, v = R[i + 2], V[i + 2]
            link = V[i + 3] + jnp.where(rowi > 0, pltpu.roll(v, 1, 0), 0.0)
            link = link + jnp.where(coli > 0, pltpu.roll(v, 1, 1), 0.0)
            av = (SIG[i] + 6.0) * v - 2.0 * link
            return (m0 + fold(r * r), m1 + fold(r * v), m2 + fold(v * v), m3 + fold(v * av))

        z8 = jnp.zeros((8, 2 * hl), F32)
        ms = lax.fori_loop(0, lx, step, (z8, z8, z8, z8))
        block = jnp.zeros((8, 2 * hl), F32)
        for j, m in enumerate(ms):
            block = jnp.where(row8 == j, jnp.sum(m, axis=0, keepdims=True), block)
        arb[stage, s] = block
        others(
            S, s, lambda d: remote(arb.at[stage, s], arb.at[stage, s], 8 + stage, (n, d)).start()
        )

    def fine_coefficients(stage):
        wait_on(arb.at[stage, pl.ds(0, S - 1)], recv.at[8 + stage])
        m = jnp.sum(jnp.sum(arb[stage], axis=0), axis=1, keepdims=True)
        m0, m1, m2, m3 = (m[j:j + 1] for j in range(4))
        q1, q2, q3 = m1 / m0, m2 / m1, m3 / m2
        gap = q3 - q2
        plain = gap <= 1e-6 * q3
        gap = jnp.where(plain, 1.0, gap)
        a = jnp.where(plain, 1.0 / q1, (q3 - q1) / (q1 * gap))
        b = jnp.where(plain, 0.0, (q1 - q2) / (q1 * q2 * gap))
        return a, b

    def halo_copies(k):
        base = 12 + 4 * k
        ups = (
            remote(R.at[lx], R.at[0], base, up_dev),
            remote(V.at[pl.ds(lx, 2)], V.at[pl.ds(0, 2)], base + 1, up_dev),
        )
        downs = (
            remote(R.at[4], R.at[lx + 4], base + 2, down_dev),
            remote(V.at[pl.ds(3, 2)], V.at[pl.ds(lx + 3, 2)], base + 3, down_dev),
        )
        return ups, downs

    def fine_run(k):
        fine_residual(0)
        fine_moments(2 * k)
        ups, downs = halo_copies(k)

        @pl.when(has_hi)
        def _():
            for c in ups:
                c.start()

        @pl.when(has_lo)
        def _():
            for c in downs:
                c.start()

        a, b = fine_coefficients(2 * k)

        @pl.when(has_hi)
        def _():
            for c in ups:
                c.wait_send()
            for c in downs:
                c.wait_recv()

        @pl.when(has_lo)
        def _():
            for c in downs:
                c.wait_send()
            for c in ups:
                c.wait_recv()

        def update(i, carry):
            U[i] = U[i] + a * R[i] + b * V[i]
            return carry

        lax.fori_loop(0, lx + 5, update, 0)
        fine_residual(1)
        fine_moments(2 * k + 1)
        a, b = fine_coefficients(2 * k + 1)

        for p in range(lx):
            value = U[p + 2] + a * R[p + 2] + b * V[p + 2]
            FE[k, p] = value
            if k == PARA_ITERS - 1:
                ends_out[0, p] = value
        for blk in range(px):
            tot = (FE[k, 4 * blk] + FE[k, 4 * blk + 1]) + (FE[k, 4 * blk + 2] + FE[k, 4 * blk + 3])
            rf[k, me * px + blk] = restrict4(tot)
        part = rf.at[k, pl.ds(me * px, px)]
        others(N, me, lambda d: remote(part, part, 20 + k, (d // S, lax.rem(d, S))).start())

    def z_copy(k):
        return remote(FE.at[k], ZB.at[k], 22 + k, (lax.rem(n + 1, T), s))

    def rf_wait(k):
        wait_on(rf.at[k, pl.ds(0, (N - 1) * px)], recv.at[20 + k])

    wait_on(setup.at[pl.ds(0, (S - 1) * px)], recv.at[0])
    wait_on(cur.at[pl.ds(0, T - 1)], recv.at[1])
    wt[...] = setup[:, 1] / float(FINE_STEPS)
    C[...] = setup[:, 0]

    def sweep0(i, carry):
        solve_step(i, 0)
        return carry

    lax.fori_loop(0, T - 1, sweep0, 0)

    prev = lax.rem(n + T - 1, T)
    below = jnp.maximum(s * px - 1, 0)
    above = jnp.minimum(s * px + px, XC - 1)

    def put_prolonged(rest):
        lo = jnp.where(has_lo, prolong(D[prev, below]), 0.0)
        hi = jnp.where(has_hi, prolong(D[prev, above]), 0.0)
        own = [prolong(D[prev, s * px + blk]) for blk in range(px)]
        for i in range(2):
            U[i] = lo + HL[i] if rest else lo
        for i in range(lx):
            U[i + 2] = own[i // 4] + ZB[0, i] if rest else own[i // 4]
        for i in range(3):
            U[lx + 2 + i] = hi + HH[i] if rest else hi

    @pl.when(has_hi)
    def _():
        c_src_up.wait_send()
        c_src_dn.wait_recv()
        c_sig_dn.wait_recv()

    @pl.when(has_lo)
    def _():
        c_src_dn.wait_send()
        c_sig_dn.wait_send()
        c_src_up.wait_recv()

    @pl.when(first)
    def _():
        @pl.when(has_hi)
        def _():
            c_ini_up.wait_send()
            c_ini_dn.wait_recv()

        @pl.when(has_lo)
        def _():
            c_ini_dn.wait_send()
            c_ini_up.wait_recv()

        for i in range(2):
            U[i] = HL[i]
        for i in range(lx):
            U[i + 2] = init[i]
        for i in range(3):
            U[lx + 2 + i] = HH[i]

    @pl.when(jnp.logical_not(first))
    def _():
        put_prolonged(False)

    fine_run(0)
    z0 = z_copy(0)
    z0.start()

    solve_step(T - 1, 0)
    solve_step(0, 1)

    rf_wait(0)

    def sweep1(i, carry):
        next_start(i - 1, 1)
        solve_step(i, 1)
        return carry

    r_up = remote(ZB.at[0, pl.ds(lx - 2, 2)], HL, 24, up_dev)
    r_dn = remote(ZB.at[0, pl.ds(0, 3)], HH, 25, down_dev)
    later = jnp.logical_not(first)

    @pl.when(later)
    def _():
        z0.wait_recv()

        @pl.when(has_hi)
        def _():
            r_up.start()

        @pl.when(has_lo)
        def _():
            r_dn.start()

    lax.fori_loop(1, T - 1, sweep1, 0)

    @pl.when(later)
    def _():
        @pl.when(has_hi)
        def _():
            r_up.wait_send()
            r_dn.wait_recv()

        @pl.when(has_lo)
        def _():
            r_dn.wait_send()
            r_up.wait_recv()

        put_prolonged(True)

    @pl.when(first)
    def _():
        put_prolonged(False)

    fine_run(1)
    z1 = z_copy(1)

    @pl.when(n < T - 1)
    def _():
        z1.start()

    next_start(T - 2, 1)
    solve_step(T - 1, 1)
    next_start(T - 1, 1)
    solve_step(0, 2)
    rf_wait(1)

    def sweep2(i, carry):
        next_start(i - 1, 2)
        solve_step(i, 2)
        return carry

    lax.fori_loop(1, T - 1, sweep2, 0)

    @pl.when(first)
    def _():
        z0.wait_recv()

    @pl.when(later)
    def _():
        z1.wait_recv()

    slot = jnp.minimum(n, 1)
    for i in range(lx):
        starts_out[0, i] = ZB[slot, i] + prolong(D[prev, s * px + i // 4])

    z0.wait_send()

    @pl.when(n < T - 1)
    def _():
        z1.wait_send()

    wait_on(setup.at[pl.ds(0, (S - 1) * px)], send.at[0])
    wait_on(cur.at[pl.ds(0, T - 1)], send.at[1])
    for stage in range(2 * PARA_ITERS):
        wait_on(arb.at[stage, pl.ds(0, S - 1)], send.at[8 + stage])
    for k in range(PARA_ITERS):
        wait_on(rf.at[k, pl.ds(0, (N - 1) * px)], send.at[20 + k])


def body(T, S, labels, conductivity, coil_pattern, currents, initial_state):
    lx, NY, NZ = initial_state.shape
    phases = coil_pattern.shape[0]
    px = lx // 4
    XC = S * px
    hr, hl = NY // 8, NZ // 4
    vm = pl.BlockSpec(memory_space=pltpu.VMEM)
    sm = pl.BlockSpec(memory_space=pltpu.SMEM)
    shape = jax.ShapeDtypeStruct((1, lx, NY, NZ), F32)
    coarse = (XC, hr, 2 * hl)

    def plane(*lead):
        return pltpu.VMEM(lead + (NY, NZ), F32)

    return pl.pallas_call(
        functools.partial(kernel, T, S, lx),
        out_shape=(shape, shape),
        in_specs=[vm, sm, vm, sm, vm],
        out_specs=(vm, vm),
        scratch_shapes=[
            pltpu.VMEM((T, 8, 2 * hl), F32),
            pltpu.VMEM((XC, 2 + phases, hr, 2 * hl), F32),
            pltpu.VMEM(coarse, F32),
            pltpu.VMEM((T,) + coarse, F32),
            pltpu.VMEM((T,) + coarse, F32),
            pltpu.VMEM(coarse, F32),
            pltpu.VMEM((PARA_ITERS, T * XC) + coarse[1:], F32),
            pltpu.VMEM((2 * PARA_ITERS, S, 8, 2 * hl), F32),
            plane(lx + 5),
            plane(lx + 5),
            plane(lx + 5),
            plane(FINE_STEPS, lx + 3),
            plane(lx + 1),
            plane(2),
            plane(3),
            plane(PARA_ITERS, lx),
            plane(PARA_ITERS, lx),
            pltpu.SemaphoreType.DMA((26,)),
            pltpu.SemaphoreType.DMA((26,)),
        ],
        compiler_params=pltpu.CompilerParams(
            collective_id=0, has_side_effects=True, vmem_limit_bytes=56 * 1024 * 1024
        ),
    )(labels, conductivity, coil_pattern, currents, initial_state)


def solution(mesh):
    T, S = mesh.shape["tm"], mesh.shape["space"]
    in_specs = (
        P("space", None, None),
        P(),
        P(None, "space", None, None),
        P("tm", None, None),
        P("space", None, None),
    )
    out_specs = (P("tm", "space", None, None), P("tm", "space", None, None))
    return jax.shard_map(
        functools.partial(body, T, S), mesh=mesh, in_specs=in_specs, out_specs=out_specs,
        check_vma=False,
    )
```

```python
import functools

import jax
import jax.numpy as jnp
from jax import lax
from jax.experimental import pallas as pl
from jax.experimental.pallas import tpu as pltpu
from jax.sharding import PartitionSpec as P

FINE_STEPS = 2
CG_COARSE = 4
PARA_ITERS = 2
MESH = pl.DeviceIdType.MESH
HIGH = lax.Precision.HIGHEST
F32 = jnp.float32


def dot(a, b):
    return lax.dot_general(
        a, b, (((1,), (0,)), ((), ())), precision=HIGH, preferred_element_type=F32
    )


def kernel(
    T, S, lx, labels_in, cond, coil_in, currents, init_in, starts_out, ends_out,
    cur, setup, wt, G, D, C, rf, arb, U, R, V, coil, labels, init, SIG, HL, HH, ZB, FE,
    send, recv, load,
):
    NY, NZ = init.shape[1], init.shape[2]
    loads = [
        pltpu.make_async_copy(init_in, init, load.at[0]),
        pltpu.make_async_copy(labels_in, labels, load.at[1]),
        pltpu.make_async_copy(coil_in, coil.at[:, pl.ds(1, lx)], load.at[2]),
    ]
    for c in loads:
        c.start()
    px = lx // 4
    XC = S * px
    hr, hl = NY // 8, NZ // 4
    N = T * S
    n = lax.axis_index("tm")
    s = lax.axis_index("space")
    me = n * S + s
    has_lo, has_hi = s > 0, s < S - 1
    phases = coil.shape[0]

    prev = lax.rem(n + T - 1, T)

    def others(count, own, fn):
        for i in range(1, count):
            fn(lax.rem(own + i, count))

    def everyone(fn):
        def step(j, carry):
            dn = lax.rem(n + j, T)
            for i in range(S):
                fn(dn, lax.rem(s + i, S))
            return carry

        lax.fori_loop(1, T, step, 0)
        others(S, s, lambda d: fn(n, d))

    barrier = pltpu.get_barrier_semaphore()
    everyone(
        lambda dn, d: pl.semaphore_signal(
            barrier, inc=1, device_id=(dn, d), device_id_type=MESH
        )
    )

    def remote(src, dst, i, dev):
        return pltpu.make_async_remote_copy(
            src_ref=src, dst_ref=dst, send_sem=send.at[i], recv_sem=recv.at[i],
            device_id=dev, device_id_type=MESH,
        )

    def wait_on(ref, sem):
        pltpu.make_async_copy(ref, ref, sem).wait()

    up_dev, down_dev = (n, s + 1), (n, s - 1)

    rowi = lax.broadcasted_iota(jnp.int32, (NY, NZ), 0)
    coli = lax.broadcasted_iota(jnp.int32, (NY, NZ), 1)
    ey = (lax.broadcasted_iota(jnp.int32, (NY // 4, NY), 1) // 4
          == lax.broadcasted_iota(jnp.int32, (NY // 4, NY), 0)).astype(F32)
    eyt = (lax.broadcasted_iota(jnp.int32, (NY, NY // 4), 0) // 4
           == lax.broadcasted_iota(jnp.int32, (NY, NY // 4), 1)).astype(F32)
    zr = lax.broadcasted_iota(jnp.int32, (NZ, 2 * hl), 0) // 4
    zc = lax.broadcasted_iota(jnp.int32, (NZ, 2 * hl), 1)
    down_lo = (zr == zc).astype(F32)
    down_hi = (zr == zc - hl).astype(F32)
    tr = lax.broadcasted_iota(jnp.int32, (2 * hl, NZ), 0)
    tc = lax.broadcasted_iota(jnp.int32, (2 * hl, NZ), 1) // 4
    up_lo = (tr == tc).astype(F32)
    up_hi = (tr - hl == tc).astype(F32)

    def restrict4(total):
        t = dot(ey, total)
        return (dot(t[:hr], down_lo) + dot(t[hr:], down_hi)) * (1.0 / 64.0)

    def prolong(c):
        t = jnp.concatenate([dot(c, up_lo), dot(c, up_hi)], axis=0)
        return dot(eyt, t)

    def beside_yz(x):
        a = jnp.where(rowi > 0, pltpu.roll(x, 1, 0), 0.0)
        b = jnp.where(rowi < NY - 1, pltpu.roll(x, NY - 1, 0), 0.0)
        c = jnp.where(coli > 0, pltpu.roll(x, 1, 1), 0.0)
        d = jnp.where(coli < NZ - 1, pltpu.roll(x, NZ - 1, 1), 0.0)
        return (a + b) + (c + d)

    for c in loads:
        c.wait()
    for p in range(lx):
        lab = labels[p]
        sig = jnp.where(lab == 0, cond[0], 0.0)
        for region in range(1, cond.shape[0]):
            sig = jnp.where(lab == region, cond[region], sig)
        SIG[p] = sig

    for b in range(px):
        def total(get):
            return (get(4 * b) + get(4 * b + 1)) + (get(4 * b + 2) + get(4 * b + 3))

        setup[s * px + b, 0] = restrict4(total(lambda p: init[p]))
        setup[s * px + b, 1] = restrict4(total(lambda p: SIG[p]))
        for ph in range(phases):
            setup[s * px + b, 2 + ph] = restrict4(total(lambda p, ph=ph: coil[ph, p + 1]))
    row8 = lax.broadcasted_iota(jnp.int32, (8, 2 * hl), 0)
    row16 = lax.broadcasted_iota(jnp.int32, (16, 2 * hl), 0)
    rows = jnp.zeros((16, 2 * hl), F32)
    for ph in range(phases):
        m = currents[0, 0, ph]
        for f in range(1, FINE_STEPS):
            m = m + currents[0, f, ph]
        rows = jnp.where(row16 == ph, m / float(FINE_STEPS), rows)
        for f in range(FINE_STEPS):
            rows = jnp.where(row16 == phases * (1 + f) + ph, currents[0, f, ph], rows)
    cur[n] = rows

    zero = jnp.zeros((NY, NZ), F32)

    @pl.when(jnp.logical_not(has_lo))
    def _():
        for ref, ids in ((HL.at[0], (0, 1)), (HL.at[1], (0, 1)), (R, (0,)), (V, (0, 1))):
            for i in ids:
                ref[i] = zero
        for ph in range(phases):
            coil[ph, 0] = zero

    @pl.when(jnp.logical_not(has_hi))
    def _():
        for ref, ids in (
            (HH.at[0], (0, 1, 2)), (HH.at[1], (0, 1, 2)),
            (R, (lx + 4,)), (V, (lx + 3, lx + 4)), (SIG, (lx,)),
        ):
            for i in ids:
                ref[i] = zero
        for ph in range(phases):
            coil[ph, lx + 1] = zero
            coil[ph, lx + 2] = zero

    pl.semaphore_wait(barrier, N - 1)

    mine = setup.at[pl.ds(s * px, px)]
    others(T, n, lambda d: remote(cur.at[n], cur.at[n], 1, (d, s)).start())
    others(S, s, lambda d: remote(mine, mine, 0, (n, d)).start())
    c_src_up = remote(coil.at[:, lx], coil.at[:, 0], 2, up_dev)
    c_src_dn = remote(coil.at[:, pl.ds(1, 2)], coil.at[:, pl.ds(lx + 1, 2)], 3, down_dev)
    c_sig_dn = remote(SIG.at[0], SIG.at[lx], 4, down_dev)
    c_ini_up = remote(init.at[pl.ds(lx - 2, 2)], HL.at[0], 5, up_dev)
    c_ini_dn = remote(init.at[pl.ds(0, 3)], HH.at[0], 6, down_dev)
    first = prev == 0

    @pl.when(jnp.logical_and(first, has_hi))
    def _():
        c_ini_up.start()

    @pl.when(jnp.logical_and(first, has_lo))
    def _():
        c_ini_dn.start()

    @pl.when(has_hi)
    def _():
        c_src_up.start()

    @pl.when(has_lo)
    def _():
        c_src_dn.start()
        c_sig_dn.start()

    crow = lax.broadcasted_iota(jnp.int32, (XC, hr, 2 * hl), 1)
    ccol = lax.broadcasted_iota(jnp.int32, (XC, hr, 2 * hl), 2)
    cz = lax.rem(ccol, hl)
    zplane = jnp.zeros((1, hr, 2 * hl), F32)

    def coarse_lap(c):
        xs = jnp.concatenate([zplane, c[:-1]], 0) + jnp.concatenate([c[1:], zplane], 0)
        w = pltpu.roll(c, hl, 2)
        za = jnp.where(cz > 0, pltpu.roll(c, 1, 2), 0.0)
        zb = jnp.where(cz < hl - 1, pltpu.roll(c, 2 * hl - 1, 2), 0.0)
        ya = pltpu.roll(
            jnp.where(crow == hr - 1, jnp.where(ccol >= hl, w, 0.0), c), 1, 1)
        yb = pltpu.roll(
            jnp.where(crow == 0, jnp.where(ccol < hl, w, 0.0), c), hr - 1, 1)
        return 0.0625 * (6.0 * c - ((xs + za) + (zb + ya) + yb))

    def total3(x):
        return jnp.sum(jnp.sum(x, axis=0), keepdims=True).reshape(1, 1, 1)

    def solve(i, c):
        source = cur[i, 0:1, :][None] * setup[:, 2]
        for ph in range(1, phases):
            source = source + cur[i, ph:ph + 1, :][None] * setup[:, 2 + ph]
        weight = wt[...]
        r = source - coarse_lap(c)
        q = weight * r + coarse_lap(r)
        rr, rq = total3(r * r), total3(r * q)
        alpha = rr / rq
        d, x = r, c
        for it in range(CG_COARSE):
            x = x + alpha * d
            if it + 1 < CG_COARSE:
                r = r - alpha * q
                w = weight * r + coarse_lap(r)
                new, rw = total3(r * r), total3(r * w)
                beta = new / rr
                alpha = new / (rw - beta * new / alpha)
                d = r + beta * d
                q = w + beta * q
                rr = new
        return x

    def solve_step(i, k):
        g = solve(i, C[...])
        if k == 0:
            D[i] = g
            C[...] = g
        else:
            diff = g - G[i]
            D[i] = diff
        G[i] = g

    def next_start(i, k):
        C[...] = D[i] + rf[k - 1, pl.ds(i * XC, XC)]

    def fine_residual(f, sl):
        amps = [
            cur[sl, phases * (1 + f) + ph:phases * (1 + f) + ph + 1, 0:1] for ph in range(phases)
        ]

        def step(i, carry):
            g = s * lx + i - 1
            u = U[i + 1]
            source = amps[0] * coil[0, i]
            for ph in range(1, phases):
                source = source + amps[ph] * coil[ph, i]
            r = source - 6.0 * u + ((U[i] + U[i + 2]) + beside_yz(u))
            inside = jnp.logical_and(g >= 0, g < S * lx)
            R[i + 1] = jnp.where(inside, r, 0.0)
            return carry

        lax.fori_loop(0, lx + 3, step, 0)

        def step_v(i, carry):
            g = s * lx + i
            r = R[i + 2]
            v = (SIG[i] + 6.0) * r - ((R[i + 1] + R[i + 3]) + beside_yz(r))
            V[i + 2] = jnp.where(g < S * lx, v, 0.0)
            return carry

        lax.fori_loop(0, lx + 1, step_v, 0)

    def fold(x):
        y = x[:, :2 * hl]
        for j in range(1, NZ // (2 * hl)):
            y = y + x[:, 2 * hl * j:2 * hl * (j + 1)]
        z = y[:8]
        for j in range(1, NY // 8):
            z = z + y[8 * j:8 * (j + 1)]
        return z

    def fine_moments(stage):
        def step(i, carry):
            m0, m1, m2, m3 = carry
            r, v = R[i + 2], V[i + 2]
            link = V[i + 3] + jnp.where(rowi > 0, pltpu.roll(v, 1, 0), 0.0)
            link = link + jnp.where(coli > 0, pltpu.roll(v, 1, 1), 0.0)
            av = (SIG[i] + 6.0) * v - 2.0 * link
            return (m0 + fold(r * r), m1 + fold(r * v), m2 + fold(v * v), m3 + fold(v * av))

        z8 = jnp.zeros((8, 2 * hl), F32)
        ms = lax.fori_loop(0, lx, step, (z8, z8, z8, z8))
        block = jnp.zeros((8, 2 * hl), F32)
        for j, m in enumerate(ms):
            block = jnp.where(row8 == j, jnp.sum(m, axis=0, keepdims=True), block)
        arb[stage, s] = block
        others(
            S, s, lambda d: remote(arb.at[stage, s], arb.at[stage, s], 8 + stage, (n, d)).start()
        )

    def fine_coefficients(stage):
        wait_on(arb.at[stage, pl.ds(0, S - 1)], recv.at[8 + stage])
        m = jnp.sum(jnp.sum(arb[stage], axis=0), axis=1, keepdims=True)
        m0, m1, m2, m3 = (m[j:j + 1] for j in range(4))
        q1, q2, q3 = m1 / m0, m2 / m1, m3 / m2
        gap = q3 - q2
        plain = gap <= 1e-6 * q3
        gap = jnp.where(plain, 1.0, gap)
        a = jnp.where(plain, 1.0 / q1, (q3 - q1) / (q1 * gap))
        b = jnp.where(plain, 0.0, (q1 - q2) / (q1 * q2 * gap))
        return a, b

    def halo_copies(k):
        base = 12 + 4 * k
        ups = (
            remote(R.at[lx], R.at[0], base, up_dev),
            remote(V.at[pl.ds(lx, 2)], V.at[pl.ds(0, 2)], base + 1, up_dev),
        )
        downs = (
            remote(R.at[4], R.at[lx + 4], base + 2, down_dev),
            remote(V.at[pl.ds(3, 2)], V.at[pl.ds(lx + 3, 2)], base + 3, down_dev),
        )
        return ups, downs

    def fine_run(k, sl):
        fine_residual(0, sl)
        fine_moments(2 * k)
        ups, downs = halo_copies(k)

        @pl.when(has_hi)
        def _():
            for c in ups:
                c.start()

        @pl.when(has_lo)
        def _():
            for c in downs:
                c.start()

        a, b = fine_coefficients(2 * k)

        @pl.when(has_hi)
        def _():
            for c in ups:
                c.wait_send()
            for c in downs:
                c.wait_recv()

        @pl.when(has_lo)
        def _():
            for c in downs:
                c.wait_send()
            for c in ups:
                c.wait_recv()

        def update(i, carry):
            U[i] = U[i] + a * R[i] + b * V[i]
            return carry

        lax.fori_loop(0, lx + 5, update, 0)
        fine_residual(1, sl)
        fine_moments(2 * k + 1)
        a, b = fine_coefficients(2 * k + 1)

        for p in range(lx):
            value = U[p + 2] + a * R[p + 2] + b * V[p + 2]
            FE[k, p] = value
        for blk in range(px):
            tot = (FE[k, 4 * blk] + FE[k, 4 * blk + 1]) + (FE[k, 4 * blk + 2] + FE[k, 4 * blk + 3])
            rf[k, (sl * S + s) * px + blk] = restrict4(tot)
        part = rf.at[k, pl.ds((sl * S + s) * px, px)]
        everyone(lambda dn, d: remote(part, part, 20 + k, (dn, d)).start())

    def rf_wait(k):
        wait_on(rf.at[k, pl.ds(0, (N - 1) * px)], recv.at[20 + k])

    wait_on(setup.at[pl.ds(0, (S - 1) * px)], recv.at[0])
    wait_on(cur.at[pl.ds(0, T - 1)], recv.at[1])
    wt[...] = setup[:, 1] / float(FINE_STEPS)
    C[...] = setup[:, 0]

    def sweep0(i, carry):
        solve_step(i, 0)
        return carry

    lax.fori_loop(0, T - 1, sweep0, 0)

    below = jnp.maximum(s * px - 1, 0)
    above = jnp.minimum(s * px + px, XC - 1)

    def put_prolonged(at, rest):
        lo = jnp.where(has_lo, prolong(D[at, below]), 0.0)
        hi = jnp.where(has_hi, prolong(D[at, above]), 0.0)
        own = [prolong(D[at, s * px + blk]) for blk in range(px)]
        for i in range(2):
            U[i] = lo + HL[1, i] if rest else lo
        for i in range(lx):
            U[i + 2] = own[i // 4] + FE[0, i] if rest else own[i // 4]
        for i in range(3):
            U[lx + 2 + i] = hi + HH[1, i] if rest else hi

    @pl.when(has_hi)
    def _():
        c_src_up.wait_send()
        c_src_dn.wait_recv()
        c_sig_dn.wait_recv()

    @pl.when(has_lo)
    def _():
        c_src_dn.wait_send()
        c_sig_dn.wait_send()
        c_src_up.wait_recv()

    @pl.when(first)
    def _():
        @pl.when(has_hi)
        def _():
            c_ini_up.wait_send()
            c_ini_dn.wait_recv()

        @pl.when(has_lo)
        def _():
            c_ini_dn.wait_send()
            c_ini_up.wait_recv()

        for i in range(2):
            U[i] = HL[0, i]
        for i in range(lx):
            U[i + 2] = init[i]
        for i in range(3):
            U[lx + 2 + i] = HH[0, i]

    @pl.when(jnp.logical_not(first))
    def _():
        put_prolonged(lax.rem(n + T - 2, T), False)

    fine_run(0, prev)
    later = n > 0
    r_up = remote(FE.at[0, pl.ds(lx - 2, 2)], HL.at[1], 24, up_dev)
    r_dn = remote(FE.at[0, pl.ds(0, 3)], HH.at[1], 25, down_dev)

    @pl.when(jnp.logical_and(later, has_hi))
    def _():
        r_up.start()

    @pl.when(jnp.logical_and(later, has_lo))
    def _():
        r_dn.start()

    solve_step(T - 1, 0)
    solve_step(0, 1)

    rf_wait(0)

    def sweep1(i, carry):
        next_start(i - 1, 1)
        solve_step(i, 1)
        return carry

    lax.fori_loop(1, T - 1, sweep1, 0)

    @pl.when(later)
    def _():
        @pl.when(has_hi)
        def _():
            r_up.wait_send()
            r_dn.wait_recv()

        @pl.when(has_lo)
        def _():
            r_dn.wait_send()
            r_up.wait_recv()

        put_prolonged(prev, True)

    @pl.when(jnp.logical_not(later))
    def _():
        put_prolonged(prev, False)

    fine_run(1, n)
    z1 = remote(FE.at[1], ZB, 22, (lax.rem(n + 1, T), s))
    put_ends = pltpu.make_async_copy(FE.at[1], ends_out.at[0], load.at[0])
    put_ends.start()

    @pl.when(n < T - 1)
    def _():
        z1.start()

    next_start(T - 2, 1)
    solve_step(T - 1, 1)
    next_start(T - 1, 1)
    solve_step(0, 2)
    rf_wait(1)

    def sweep2(i, carry):
        next_start(i - 1, 2)
        solve_step(i, 2)
        return carry

    lax.fori_loop(1, T - 1, sweep2, 0)

    @pl.when(later)
    def _():
        z1.wait_recv()
        for i in range(lx):
            U[i] = ZB[i] + prolong(D[prev, s * px + i // 4])

    @pl.when(jnp.logical_not(later))
    def _():
        for i in range(lx):
            U[i] = FE[0, i] + prolong(D[prev, s * px + i // 4])

    put_starts = pltpu.make_async_copy(U.at[pl.ds(0, lx)], starts_out.at[0], load.at[1])
    put_starts.start()

    @pl.when(n < T - 1)
    def _():
        z1.wait_send()

    wait_on(setup.at[pl.ds(0, (S - 1) * px)], send.at[0])
    wait_on(cur.at[pl.ds(0, T - 1)], send.at[1])
    for stage in range(2 * PARA_ITERS):
        wait_on(arb.at[stage, pl.ds(0, S - 1)], send.at[8 + stage])
    for k in range(PARA_ITERS):
        wait_on(rf.at[k, pl.ds(0, (N - 1) * px)], send.at[20 + k])
    put_ends.wait()
    put_starts.wait()


def body(T, S, labels, conductivity, coil_pattern, currents, initial_state):
    lx, NY, NZ = initial_state.shape
    phases = coil_pattern.shape[0]
    px = lx // 4
    XC = S * px
    hr, hl = NY // 8, NZ // 4
    hb = pl.BlockSpec(memory_space=pl.ANY)
    sm = pl.BlockSpec(memory_space=pltpu.SMEM)
    shape = jax.ShapeDtypeStruct((1, lx, NY, NZ), F32)
    coarse = (XC, hr, 2 * hl)

    def plane(*lead):
        return pltpu.VMEM(lead + (NY, NZ), F32)

    return pl.pallas_call(
        functools.partial(kernel, T, S, lx),
        out_shape=(shape, shape),
        in_specs=[hb, sm, hb, sm, hb],
        out_specs=(hb, hb),
        scratch_shapes=[
            pltpu.VMEM((T, 16, 2 * hl), F32),
            pltpu.VMEM((XC, 2 + phases, hr, 2 * hl), F32),
            pltpu.VMEM(coarse, F32),
            pltpu.VMEM((T,) + coarse, F32),
            pltpu.VMEM((T,) + coarse, F32),
            pltpu.VMEM(coarse, F32),
            pltpu.VMEM((PARA_ITERS, T * XC) + coarse[1:], F32),
            pltpu.VMEM((2 * PARA_ITERS, S, 8, 2 * hl), F32),
            plane(lx + 5),
            plane(lx + 5),
            plane(lx + 5),
            plane(phases, lx + 3),
            pltpu.VMEM((lx, NY, NZ), labels.dtype),
            plane(lx),
            plane(lx + 1),
            plane(2, 2),
            plane(2, 3),
            plane(lx),
            plane(PARA_ITERS, lx),
            pltpu.SemaphoreType.DMA((26,)),
            pltpu.SemaphoreType.DMA((26,)),
            pltpu.SemaphoreType.DMA((3,)),
        ],
        compiler_params=pltpu.CompilerParams(
            collective_id=0, has_side_effects=True, vmem_limit_bytes=56 * 1024 * 1024
        ),
    )(labels, conductivity, coil_pattern, currents, initial_state)


def solution(mesh):
    T, S = mesh.shape["tm"], mesh.shape["space"]
    in_specs = (
        P("space", None, None),
        P(),
        P(None, "space", None, None),
        P("tm", None, None),
        P("space", None, None),
    )
    out_specs = (P("tm", "space", None, None), P("tm", "space", None, None))
    return jax.shard_map(
        functools.partial(body, T, S), mesh=mesh, in_specs=in_specs, out_specs=out_specs,
        check_vma=False,
    )
```

```python
import functools

import jax
import jax.numpy as jnp
from jax import lax
from jax.experimental import pallas as pl
from jax.experimental.pallas import tpu as pltpu
from jax.sharding import PartitionSpec as P

FINE_STEPS = 2
CG_COARSE = 4
PARA_ITERS = 2
MESH = pl.DeviceIdType.MESH
F32 = jnp.float32
BF16 = jnp.bfloat16


def pieces(x):
    first = x.astype(BF16)
    x = x - first.astype(F32)
    second = x.astype(BF16)
    return first, second, (x - second.astype(F32)).astype(BF16)


def dot(a, b):
    left = pieces(a) if a.dtype == F32 else (a,) * 3
    right = pieces(b) if b.dtype == F32 else (b,) * 3
    first, second, third = (
        jnp.dot(x, y, preferred_element_type=F32) for x, y in zip(left, right)
    )
    return first + (second + third)


def kernel(
    T, S, lx, labels_in, cond, coil_in, currents, init_in, starts_out, ends_out,
    cur, setup, wt, G, D, C, rf, arb, U, R, V, coil, labels, init, SIG, HL, HH, ZB, FE,
    send, recv, load,
):
    NY, NZ = init.shape[1], init.shape[2]
    loads = [
        pltpu.make_async_copy(init_in, init, load.at[0]),
        pltpu.make_async_copy(labels_in, labels, load.at[1]),
        pltpu.make_async_copy(coil_in, coil.at[:, pl.ds(1, lx)], load.at[2]),
    ]
    for c in loads:
        c.start()
    px = lx // 4
    XC = S * px
    hr, hl = NY // 8, NZ // 4
    N = T * S
    n = lax.axis_index("tm")
    s = lax.axis_index("space")
    me = n * S + s
    has_lo, has_hi = s > 0, s < S - 1
    phases = coil.shape[0]

    prev = lax.rem(n + T - 1, T)

    def others(count, own, fn):
        for i in range(1, count):
            fn(lax.rem(own + i, count))

    def everyone(fn):
        def step(j, carry):
            dn = lax.rem(n + j, T)
            for i in range(S):
                fn(dn, lax.rem(s + i, S))
            return carry

        lax.fori_loop(1, T, step, 0)
        others(S, s, lambda d: fn(n, d))

    barrier = pltpu.get_barrier_semaphore()
    everyone(
        lambda dn, d: pl.semaphore_signal(
            barrier, inc=1, device_id=(dn, d), device_id_type=MESH
        )
    )

    def remote(src, dst, i, dev):
        return pltpu.make_async_remote_copy(
            src_ref=src, dst_ref=dst, send_sem=send.at[i], recv_sem=recv.at[i],
            device_id=dev, device_id_type=MESH,
        )

    def wait_on(ref, sem):
        pltpu.make_async_copy(ref, ref, sem).wait()

    up_dev, down_dev = (n, s + 1), (n, s - 1)

    rowi = lax.broadcasted_iota(jnp.int32, (NY, NZ), 0)
    coli = lax.broadcasted_iota(jnp.int32, (NY, NZ), 1)
    ey = (lax.broadcasted_iota(jnp.int32, (NY // 4, NY), 1) // 4
          == lax.broadcasted_iota(jnp.int32, (NY // 4, NY), 0)).astype(F32).astype(BF16)
    eyt = (lax.broadcasted_iota(jnp.int32, (NY, NY // 4), 0) // 4
           == lax.broadcasted_iota(jnp.int32, (NY, NY // 4), 1)).astype(F32).astype(BF16)
    zr = lax.broadcasted_iota(jnp.int32, (NZ, 2 * hl), 0) // 4
    zc = lax.broadcasted_iota(jnp.int32, (NZ, 2 * hl), 1)
    down_lo = (zr == zc).astype(F32).astype(BF16)
    down_hi = (zr == zc - hl).astype(F32).astype(BF16)
    tr = lax.broadcasted_iota(jnp.int32, (2 * hl, NZ), 0)
    tc = lax.broadcasted_iota(jnp.int32, (2 * hl, NZ), 1) // 4
    up_lo = (tr == tc).astype(F32).astype(BF16)
    up_hi = (tr - hl == tc).astype(F32).astype(BF16)

    def restrict4(total):
        t = dot(ey, total)
        return (dot(t[:hr], down_lo) + dot(t[hr:], down_hi)) * (1.0 / 64.0)

    def prolong(c):
        t = jnp.concatenate([dot(c, up_lo), dot(c, up_hi)], axis=0)
        return dot(eyt, t)

    def beside_yz(x):
        a = jnp.where(rowi > 0, pltpu.roll(x, 1, 0), 0.0)
        b = jnp.where(rowi < NY - 1, pltpu.roll(x, NY - 1, 0), 0.0)
        c = jnp.where(coli > 0, pltpu.roll(x, 1, 1), 0.0)
        d = jnp.where(coli < NZ - 1, pltpu.roll(x, NZ - 1, 1), 0.0)
        return (a + b) + (c + d)

    for c in loads:
        c.wait()
    for p in range(lx):
        lab = labels[p]
        sig = jnp.where(lab == 0, cond[0], 0.0)
        for region in range(1, cond.shape[0]):
            sig = jnp.where(lab == region, cond[region], sig)
        SIG[p] = sig

    for b in range(px):
        def total(get):
            return (get(4 * b) + get(4 * b + 1)) + (get(4 * b + 2) + get(4 * b + 3))

        setup[s * px + b, 0] = restrict4(total(lambda p: init[p]))
        setup[s * px + b, 1] = restrict4(total(lambda p: SIG[p]))
        for ph in range(phases):
            setup[s * px + b, 2 + ph] = restrict4(total(lambda p, ph=ph: coil[ph, p + 1]))
    row8 = lax.broadcasted_iota(jnp.int32, (8, 2 * hl), 0)
    row16 = lax.broadcasted_iota(jnp.int32, (16, 2 * hl), 0)
    rows = jnp.zeros((16, 2 * hl), F32)
    for ph in range(phases):
        m = currents[0, 0, ph]
        for f in range(1, FINE_STEPS):
            m = m + currents[0, f, ph]
        rows = jnp.where(row16 == ph, m / float(FINE_STEPS), rows)
        for f in range(FINE_STEPS):
            rows = jnp.where(row16 == phases * (1 + f) + ph, currents[0, f, ph], rows)
    cur[n] = rows

    zero = jnp.zeros((NY, NZ), F32)

    @pl.when(jnp.logical_not(has_lo))
    def _():
        for ref, ids in ((HL.at[0], (0, 1)), (HL.at[1], (0, 1)), (R, (0,)), (V, (0, 1))):
            for i in ids:
                ref[i] = zero
        for ph in range(phases):
            coil[ph, 0] = zero

    @pl.when(jnp.logical_not(has_hi))
    def _():
        for ref, ids in (
            (HH.at[0], (0, 1, 2)), (HH.at[1], (0, 1, 2)),
            (R, (lx + 4,)), (V, (lx + 3, lx + 4)), (SIG, (lx,)),
        ):
            for i in ids:
                ref[i] = zero
        for ph in range(phases):
            coil[ph, lx + 1] = zero
            coil[ph, lx + 2] = zero

    pl.semaphore_wait(barrier, N - 1)

    mine = setup.at[pl.ds(s * px, px)]
    others(T, n, lambda d: remote(cur.at[n], cur.at[n], 1, (d, s)).start())
    others(S, s, lambda d: remote(mine, mine, 0, (n, d)).start())
    c_src_up = remote(coil.at[:, lx], coil.at[:, 0], 2, up_dev)
    c_src_dn = remote(coil.at[:, pl.ds(1, 2)], coil.at[:, pl.ds(lx + 1, 2)], 3, down_dev)
    c_sig_dn = remote(SIG.at[0], SIG.at[lx], 4, down_dev)
    c_ini_up = remote(init.at[pl.ds(lx - 2, 2)], HL.at[0], 5, up_dev)
    c_ini_dn = remote(init.at[pl.ds(0, 3)], HH.at[0], 6, down_dev)
    first = prev == 0

    @pl.when(jnp.logical_and(first, has_hi))
    def _():
        c_ini_up.start()

    @pl.when(jnp.logical_and(first, has_lo))
    def _():
        c_ini_dn.start()

    @pl.when(has_hi)
    def _():
        c_src_up.start()

    @pl.when(has_lo)
    def _():
        c_src_dn.start()
        c_sig_dn.start()

    crow = lax.broadcasted_iota(jnp.int32, (XC, hr, 2 * hl), 1)
    ccol = lax.broadcasted_iota(jnp.int32, (XC, hr, 2 * hl), 2)
    cz = lax.rem(ccol, hl)
    zplane = jnp.zeros((1, hr, 2 * hl), F32)

    def coarse_lap(c):
        xs = jnp.concatenate([zplane, c[:-1]], 0) + jnp.concatenate([c[1:], zplane], 0)
        w = pltpu.roll(c, hl, 2)
        za = jnp.where(cz > 0, pltpu.roll(c, 1, 2), 0.0)
        zb = jnp.where(cz < hl - 1, pltpu.roll(c, 2 * hl - 1, 2), 0.0)
        ya = pltpu.roll(
            jnp.where(crow == hr - 1, jnp.where(ccol >= hl, w, 0.0), c), 1, 1)
        yb = pltpu.roll(
            jnp.where(crow == 0, jnp.where(ccol < hl, w, 0.0), c), hr - 1, 1)
        return 0.0625 * (6.0 * c - ((xs + za) + (zb + ya) + yb))

    def total3(x):
        y = jnp.sum(jnp.sum(x, axis=0), axis=0, keepdims=True)
        return jnp.sum(y, axis=1, keepdims=True)[None]

    def solve(i, c):
        source = cur[i, 0:1, :][None] * setup[:, 2]
        for ph in range(1, phases):
            source = source + cur[i, ph:ph + 1, :][None] * setup[:, 2 + ph]
        weight = wt[...]
        r = source - coarse_lap(c)
        q = weight * r + coarse_lap(r)
        rr, rq = total3(r * r), total3(r * q)
        alpha = rr / rq
        d, x = r, c
        for it in range(CG_COARSE):
            x = x + alpha * d
            if it + 1 < CG_COARSE:
                r = r - alpha * q
                w = weight * r + coarse_lap(r)
                new, rw = total3(r * r), total3(r * w)
                beta = new / rr
                alpha = new / (rw - beta * new / alpha)
                d = r + beta * d
                q = w + beta * q
                rr = new
        return x

    def solve_step(i, k):
        g = solve(i, C[...])
        if k == 0:
            D[i] = g
            C[...] = g
        else:
            diff = g - G[i]
            D[i] = diff
        G[i] = g

    def next_start(i, k):
        C[...] = D[i] + rf[k - 1, pl.ds(i * XC, XC)]

    def fine_residual(f, sl):
        amps = [
            cur[sl, phases * (1 + f) + ph:phases * (1 + f) + ph + 1, 0:1] for ph in range(phases)
        ]

        def step(i, carry):
            g = s * lx + i - 1
            u = U[i + 1]
            source = amps[0] * coil[0, i]
            for ph in range(1, phases):
                source = source + amps[ph] * coil[ph, i]
            r = source - 6.0 * u + ((U[i] + U[i + 2]) + beside_yz(u))
            inside = jnp.logical_and(g >= 0, g < S * lx)
            R[i + 1] = jnp.where(inside, r, 0.0)
            return carry

        lax.fori_loop(0, lx + 3, step, 0, unroll=True)

        def step_v(i, carry):
            g = s * lx + i
            r = R[i + 2]
            v = (SIG[i] + 6.0) * r - ((R[i + 1] + R[i + 3]) + beside_yz(r))
            V[i + 2] = jnp.where(g < S * lx, v, 0.0)
            return carry

        lax.fori_loop(0, lx + 1, step_v, 0, unroll=True)

    def fold(x):
        y = x[:, :2 * hl]
        for j in range(1, NZ // (2 * hl)):
            y = y + x[:, 2 * hl * j:2 * hl * (j + 1)]
        z = y[:8]
        for j in range(1, NY // 8):
            z = z + y[8 * j:8 * (j + 1)]
        return z

    def fine_moments(stage):
        def step(i, carry):
            m0, m1, m2, m3 = carry
            r, v = R[i + 2], V[i + 2]
            link = V[i + 3] + jnp.where(rowi > 0, pltpu.roll(v, 1, 0), 0.0)
            link = link + jnp.where(coli > 0, pltpu.roll(v, 1, 1), 0.0)
            av = (SIG[i] + 6.0) * v - 2.0 * link
            return (m0 + fold(r * r), m1 + fold(r * v), m2 + fold(v * v), m3 + fold(v * av))

        z8 = jnp.zeros((8, 2 * hl), F32)
        ms = lax.fori_loop(0, lx, step, (z8, z8, z8, z8), unroll=True)
        block = jnp.zeros((8, 2 * hl), F32)
        for j, m in enumerate(ms):
            block = jnp.where(row8 == j, jnp.sum(m, axis=0, keepdims=True), block)
        arb[stage, s] = block
        others(
            S, s, lambda d: remote(arb.at[stage, s], arb.at[stage, s], 8 + stage, (n, d)).start()
        )

    def fine_coefficients(stage):
        wait_on(arb.at[stage, pl.ds(0, S - 1)], recv.at[8 + stage])
        m = jnp.sum(jnp.sum(arb[stage], axis=0), axis=1, keepdims=True)
        m0, m1, m2, m3 = (m[j:j + 1] for j in range(4))
        q1, q2, q3 = m1 / m0, m2 / m1, m3 / m2
        gap = q3 - q2
        plain = gap <= 1e-6 * q3
        gap = jnp.where(plain, 1.0, gap)
        a = jnp.where(plain, 1.0 / q1, (q3 - q1) / (q1 * gap))
        b = jnp.where(plain, 0.0, (q1 - q2) / (q1 * q2 * gap))
        return a, b

    def halo_copies(k):
        base = 12 + 4 * k
        ups = (
            remote(R.at[lx], R.at[0], base, up_dev),
            remote(V.at[pl.ds(lx, 2)], V.at[pl.ds(0, 2)], base + 1, up_dev),
        )
        downs = (
            remote(R.at[4], R.at[lx + 4], base + 2, down_dev),
            remote(V.at[pl.ds(3, 2)], V.at[pl.ds(lx + 3, 2)], base + 3, down_dev),
        )
        return ups, downs

    def fine_run(k, sl):
        fine_residual(0, sl)
        fine_moments(2 * k)
        ups, downs = halo_copies(k)

        @pl.when(has_hi)
        def _():
            for c in ups:
                c.start()

        @pl.when(has_lo)
        def _():
            for c in downs:
                c.start()

        a, b = fine_coefficients(2 * k)

        @pl.when(has_hi)
        def _():
            for c in ups:
                c.wait_send()
            for c in downs:
                c.wait_recv()

        @pl.when(has_lo)
        def _():
            for c in downs:
                c.wait_send()
            for c in ups:
                c.wait_recv()

        def update(i, carry):
            U[i] = U[i] + a * R[i] + b * V[i]
            return carry

        lax.fori_loop(0, lx + 5, update, 0, unroll=True)
        fine_residual(1, sl)
        fine_moments(2 * k + 1)
        a, b = fine_coefficients(2 * k + 1)

        for p in range(lx):
            value = U[p + 2] + a * R[p + 2] + b * V[p + 2]
            FE[k, p] = value
        for blk in range(px):
            tot = (FE[k, 4 * blk] + FE[k, 4 * blk + 1]) + (FE[k, 4 * blk + 2] + FE[k, 4 * blk + 3])
            rf[k, (sl * S + s) * px + blk] = restrict4(tot)
        part = rf.at[k, pl.ds((sl * S + s) * px, px)]
        everyone(lambda dn, d: remote(part, part, 20 + k, (dn, d)).start())

    def rf_wait(k):
        wait_on(rf.at[k, pl.ds(0, (N - 1) * px)], recv.at[20 + k])

    wait_on(setup.at[pl.ds(0, (S - 1) * px)], recv.at[0])
    wait_on(cur.at[pl.ds(0, T - 1)], recv.at[1])
    wt[...] = setup[:, 1] / float(FINE_STEPS)
    C[...] = setup[:, 0]

    def sweep0(i, carry):
        solve_step(i, 0)
        return carry

    lax.fori_loop(0, T - 1, sweep0, 0)

    below = jnp.maximum(s * px - 1, 0)
    above = jnp.minimum(s * px + px, XC - 1)

    def put_prolonged(at, rest):
        lo = jnp.where(has_lo, prolong(D[at, below]), 0.0)
        hi = jnp.where(has_hi, prolong(D[at, above]), 0.0)
        own = [prolong(D[at, s * px + blk]) for blk in range(px)]
        for i in range(2):
            U[i] = lo + HL[1, i] if rest else lo
        for i in range(lx):
            U[i + 2] = own[i // 4] + FE[0, i] if rest else own[i // 4]
        for i in range(3):
            U[lx + 2 + i] = hi + HH[1, i] if rest else hi

    @pl.when(has_hi)
    def _():
        c_src_up.wait_send()
        c_src_dn.wait_recv()
        c_sig_dn.wait_recv()

    @pl.when(has_lo)
    def _():
        c_src_dn.wait_send()
        c_sig_dn.wait_send()
        c_src_up.wait_recv()

    @pl.when(first)
    def _():
        @pl.when(has_hi)
        def _():
            c_ini_up.wait_send()
            c_ini_dn.wait_recv()

        @pl.when(has_lo)
        def _():
            c_ini_dn.wait_send()
            c_ini_up.wait_recv()

        for i in range(2):
            U[i] = HL[0, i]
        for i in range(lx):
            U[i + 2] = init[i]
        for i in range(3):
            U[lx + 2 + i] = HH[0, i]

    @pl.when(jnp.logical_not(first))
    def _():
        put_prolonged(lax.rem(n + T - 2, T), False)

    fine_run(0, prev)
    later = n > 0
    r_up = remote(FE.at[0, pl.ds(lx - 2, 2)], HL.at[1], 24, up_dev)
    r_dn = remote(FE.at[0, pl.ds(0, 3)], HH.at[1], 25, down_dev)

    @pl.when(jnp.logical_and(later, has_hi))
    def _():
        r_up.start()

    @pl.when(jnp.logical_and(later, has_lo))
    def _():
        r_dn.start()

    solve_step(T - 1, 0)
    solve_step(0, 1)

    rf_wait(0)

    def sweep1(i, carry):
        next_start(i - 1, 1)
        solve_step(i, 1)
        return carry

    lax.fori_loop(1, T - 1, sweep1, 0)

    @pl.when(later)
    def _():
        @pl.when(has_hi)
        def _():
            r_up.wait_send()
            r_dn.wait_recv()

        @pl.when(has_lo)
        def _():
            r_dn.wait_send()
            r_up.wait_recv()

        put_prolonged(prev, True)

    @pl.when(jnp.logical_not(later))
    def _():
        put_prolonged(prev, False)

    fine_run(1, n)
    z1 = remote(FE.at[1], ZB, 22, (lax.rem(n + 1, T), s))
    put_ends = pltpu.make_async_copy(FE.at[1], ends_out.at[0], load.at[0])
    put_ends.start()

    @pl.when(n < T - 1)
    def _():
        z1.start()

    next_start(T - 2, 1)
    solve_step(T - 1, 1)
    next_start(T - 1, 1)
    solve_step(0, 2)
    rf_wait(1)

    def sweep2(i, carry):
        next_start(i - 1, 2)
        solve_step(i, 2)
        return carry

    lax.fori_loop(1, T - 1, sweep2, 0)

    @pl.when(later)
    def _():
        z1.wait_recv()
        for i in range(lx):
            U[i] = ZB[i] + prolong(D[prev, s * px + i // 4])

    @pl.when(jnp.logical_not(later))
    def _():
        for i in range(lx):
            U[i] = FE[0, i] + prolong(D[prev, s * px + i // 4])

    put_starts = pltpu.make_async_copy(U.at[pl.ds(0, lx)], starts_out.at[0], load.at[1])
    put_starts.start()

    @pl.when(n < T - 1)
    def _():
        z1.wait_send()

    wait_on(setup.at[pl.ds(0, (S - 1) * px)], send.at[0])
    wait_on(cur.at[pl.ds(0, T - 1)], send.at[1])
    for stage in range(2 * PARA_ITERS):
        wait_on(arb.at[stage, pl.ds(0, S - 1)], send.at[8 + stage])
    for k in range(PARA_ITERS):
        wait_on(rf.at[k, pl.ds(0, (N - 1) * px)], send.at[20 + k])
    put_ends.wait()
    put_starts.wait()


def body(T, S, labels, conductivity, coil_pattern, currents, initial_state):
    lx, NY, NZ = initial_state.shape
    phases = coil_pattern.shape[0]
    px = lx // 4
    XC = S * px
    hr, hl = NY // 8, NZ // 4
    hb = pl.BlockSpec(memory_space=pl.ANY)
    sm = pl.BlockSpec(memory_space=pltpu.SMEM)
    shape = jax.ShapeDtypeStruct((1, lx, NY, NZ), F32)
    coarse = (XC, hr, 2 * hl)

    def plane(*lead):
        return pltpu.VMEM(lead + (NY, NZ), F32)

    return pl.pallas_call(
        functools.partial(kernel, T, S, lx),
        out_shape=(shape, shape),
        in_specs=[hb, sm, hb, sm, hb],
        out_specs=(hb, hb),
        scratch_shapes=[
            pltpu.VMEM((T, 16, 2 * hl), F32),
            pltpu.VMEM((XC, 2 + phases, hr, 2 * hl), F32),
            pltpu.VMEM(coarse, F32),
            pltpu.VMEM((T,) + coarse, F32),
            pltpu.VMEM((T,) + coarse, F32),
            pltpu.VMEM(coarse, F32),
            pltpu.VMEM((PARA_ITERS, T * XC) + coarse[1:], F32),
            pltpu.VMEM((2 * PARA_ITERS, S, 8, 2 * hl), F32),
            plane(lx + 5),
            plane(lx + 5),
            plane(lx + 5),
            plane(phases, lx + 3),
            pltpu.VMEM((lx, NY, NZ), labels.dtype),
            plane(lx),
            plane(lx + 1),
            plane(2, 2),
            plane(2, 3),
            plane(lx),
            plane(PARA_ITERS, lx),
            pltpu.SemaphoreType.DMA((26,)),
            pltpu.SemaphoreType.DMA((26,)),
            pltpu.SemaphoreType.DMA((3,)),
        ],
        compiler_params=pltpu.CompilerParams(
            collective_id=0, has_side_effects=True, vmem_limit_bytes=56 * 1024 * 1024
        ),
    )(labels, conductivity, coil_pattern, currents, initial_state)


def solution(mesh):
    T, S = mesh.shape["tm"], mesh.shape["space"]
    in_specs = (
        P("space", None, None),
        P(),
        P(None, "space", None, None),
        P("tm", None, None),
        P("space", None, None),
    )
    out_specs = (P("tm", "space", None, None), P("tm", "space", None, None))
    return jax.shard_map(
        functools.partial(body, T, S), mesh=mesh, in_specs=in_specs, out_specs=out_specs,
        check_vma=False,
    )
```
